32 devices in a mesh: energy: 2 (over y), slab: 16 (over z, x, core).
Axes of the slice: x: 2, y: 2, z: 4, core: 2. Of those that a mesh axis runs over, the one named last changes fastest.
Arguments:
- slab_green: bfloat16 [2, 128, 128, 128], P(None, ('energy', 'slab')), parts along dimension 1, may hold values from -1 to 1, as said below
- coupling: bfloat16 [2, 128, 128, 128], P(None, ('energy', 'slab')), parts along dimension 1, may hold values from -40 to 40
- left_lead_surface: bfloat16 [4, 128, 128], P('energy'), parts along dimension 0, may hold values from -8 to 8, as said below
- sigma_right: bfloat16 [4, 128, 128], P('energy'), parts along dimension 0, may hold values from -120 to 120, as said below
Outputs:
- green_diagonal: float32 [2, 128, 128, 128], P(None, ('energy', 'slab')), parts along dimension 1
The draws below stay inside these ranges and needn't reach their ends.
There are 2 independent parts, one for each index of `energy`. The reference program is written for one: setup_inputs(seed, part) draws one part's arguments, and reference() takes and returns one part's arrays. A program takes and returns all parts, laid end to end along the dimension named above; each array names one. Nothing has to cross between parts.
Inputs may be any that keep to these rules, and one draw needn't show every extreme that they name: Each block of slab_green, both parts, equals its own transpose. `left_lead_surface`: both parts equal their own transposes. `sigma_right`: both parts equal their own transposes.
All inputs are finite; a program needn't handle non-finite values.
Results may differ from the reference program's by a relative error of at most 0.035.
Values may be sent and summed in bfloat16 or wider, within the bound.
A program may use at most 128 MiB of HBM per device.

```python
import math
import jax
import jax.numpy as jnp
from jax import lax

W = 128
WIRE_LAYERS = 64


slab_scale = 0.1


def channel_draw(key):
    base = jax.random.fold_in(key, 7)
    divided_seeds = jax.random.split(base, 8)
    fraction = jax.random.uniform(divided_seeds[0], (W,), minval=0.0, maxval=1.0)
    lowest, highest = (0.7, 1.4)
    slowest = 10.0 ** (-0.3 / WIRE_LAYERS)
    fastest = 0.45
    damping_widths = fastest ** (1.0 - fraction) * slowest ** fraction
    spike_samples = jnp.where(jax.random.randint(divided_seeds[1], (WIRE_LAYERS,), 0, WIRE_LAYERS) < 3, 0.85, 1.0)
    damping_widths = damping_widths[None, :] * spike_samples[:, None]
    magnitude = jnp.exp(jax.random.uniform(divided_seeds[2], (WIRE_LAYERS, W), minval=math.log(lowest), maxval=math.log(highest)))
    first_phase = jax.random.uniform(divided_seeds[3], (WIRE_LAYERS, W), minval=-math.pi, maxval=math.pi)
    second_phase = jax.random.uniform(divided_seeds[4], (WIRE_LAYERS, W), minval=-math.pi, maxval=math.pi)
    return (damping_widths, magnitude, first_phase, second_phase, divided_seeds)


def symmetric_noise(key, shape):
    noise = jnp.clip(jax.random.normal(key, shape, jnp.float32), -5.0, 5.0)
    return (noise + jnp.swapaxes(noise, -1, -2)) / math.sqrt(2.0)


def draw_slab_green(key, part):
    damping_widths, magnitude, first_phase, second_phase, divided_seeds = channel_draw(key)
    square = jnp.eye(W, dtype=jnp.float32)
    hermitian_principal = slab_scale * magnitude * jnp.cos(first_phase)
    imag_diag = slab_scale * magnitude * jnp.sin(first_phase)
    diagonal = jnp.stack([hermitian_principal[:, None, :] * square, imag_diag[:, None, :] * square])
    noise = symmetric_noise(divided_seeds[5], (2, WIRE_LAYERS, W, W)) * (0.14 / math.sqrt(W)) * slab_scale
    return (diagonal + noise).astype(jnp.bfloat16)


def draw_coupling(key, part):
    damping_widths, magnitude, first_phase, second_phase, divided_seeds = channel_draw(key)
    square = jnp.eye(W, dtype=jnp.float32)
    total_amount = damping_widths / magnitude / slab_scale
    hermitian_principal = total_amount * jnp.cos(second_phase)
    imag_diag = total_amount * jnp.sin(second_phase)
    diagonal = jnp.stack([hermitian_principal[:, None, :] * square, imag_diag[:, None, :] * square])
    noise = jnp.clip(jax.random.normal(divided_seeds[6], (2, WIRE_LAYERS, W, W), jnp.float32), -5.0, 5.0)
    noise = noise * (0.11 / math.sqrt(W)) / slab_scale
    return (diagonal + noise).astype(jnp.bfloat16)


def lead_block(key, factor):
    divided_seeds = jax.random.split(key, 3)
    magnitude = jnp.exp(jax.random.uniform(divided_seeds[0], (W,), minval=math.log(0.5), maxval=math.log(2.0)))
    phase = jax.random.uniform(divided_seeds[1], (W,), minval=-math.pi, maxval=math.pi)
    square = jnp.eye(W, dtype=jnp.float32)
    diagonal = jnp.stack([(magnitude * jnp.cos(phase))[None, :] * square, (magnitude * jnp.sin(phase))[None, :] * square])
    noise = symmetric_noise(divided_seeds[2], (2, W, W)) * (0.14 / math.sqrt(W))
    return (factor * (diagonal + noise)).astype(jnp.bfloat16)


def draw_left_lead_surface(key, part):
    return lead_block(jax.random.fold_in(key, 31), 3.0)


def draw_sigma_right(key, part):
    return lead_block(jax.random.fold_in(key, 37), 30.0)


def setup_inputs(seed: int = 0, part: int = 0) -> dict:
    streams_of = jax.random.split(jax.random.key(seed), 5)
    own_keys = jax.random.split(jax.random.fold_in(streams_of[4], part), 5)
    return {
        "slab_green": draw_slab_green(jax.random.fold_in(jax.random.fold_in(streams_of[4], part), 71), part),
        "coupling": draw_coupling(jax.random.fold_in(jax.random.fold_in(streams_of[4], part), 71), part),
        "left_lead_surface": draw_left_lead_surface(jax.random.fold_in(jax.random.fold_in(streams_of[4], part), 71), part),
        "sigma_right": draw_sigma_right(jax.random.fold_in(jax.random.fold_in(streams_of[4], part), 71), part),
    }


def complex_product(left, right):
    real_part = jnp.dot(left[0], right[0], preferred_element_type=jnp.float32) - jnp.dot(left[1], right[1], preferred_element_type=jnp.float32)
    imag_part = jnp.dot(left[0], right[1], preferred_element_type=jnp.float32) + jnp.dot(left[1], right[0], preferred_element_type=jnp.float32)
    return jnp.stack([real_part, imag_part])


def times_transpose(left, right):
    random_numbers = (((1,), (1,)), ((), ()))
    real_part = lax.dot_general(left[0], right[0], random_numbers, preferred_element_type=jnp.float32) - lax.dot_general(left[1], right[1], random_numbers, preferred_element_type=jnp.float32)
    imag_part = lax.dot_general(left[0], right[1], random_numbers, preferred_element_type=jnp.float32) + lax.dot_general(left[1], right[0], random_numbers, preferred_element_type=jnp.float32)
    return jnp.stack([real_part, imag_part])


def sandwich(factor, current):
    inner = complex_product(factor, current.astype(jnp.bfloat16)).astype(jnp.bfloat16)
    return times_transpose(inner, factor)


def reference(slab_green, coupling, left_lead_surface, sigma_right):
    greens = jnp.moveaxis(slab_green, 1, 0)
    links = jnp.moveaxis(coupling, 1, 0)
    follow = jnp.concatenate([links[1:], links[:1]], axis=0)
    position = jnp.arange(WIRE_LAYERS, dtype=jnp.int32)

    def forward_step(current, element):
        block, link = element
        factor = times_transpose(block, link).astype(jnp.bfloat16)
        updated = sandwich(factor, current) + block.astype(jnp.float32)
        return updated, updated

    def backward_step(current, element):
        block, link, place = element
        factor = jnp.where(place == WIRE_LAYERS - 1, block, complex_product(block, link).astype(jnp.bfloat16))
        updated = sandwich(factor, current) + block.astype(jnp.float32)
        return updated, updated

    unused, left_connected = lax.scan(forward_step, left_lead_surface.astype(jnp.float32), (greens, links))
    unused2, right_connected = lax.scan(backward_step, sigma_right.astype(jnp.float32), (greens, follow, position), reverse=True)
    result = left_connected + right_connected - greens.astype(jnp.float32)
    return jnp.moveaxis(result, 0, 1)
```

```python
import functools

import jax
import jax.numpy as jnp
from jax import lax
from jax.experimental import pallas as pl
from jax.experimental.pallas import tpu as pltpu
from jax.sharding import PartitionSpec as P

MESH = pl.DeviceIdType.MESH
BF = jnp.bfloat16
F32 = jnp.float32


def wide(value):
    return jnp.concatenate([value[0], value[1]], axis=1)


def halves(out):
    width = out.shape[1] // 2
    return out[:, :width], out[:, width:]


def low(value):
    return value[0].astype(BF), value[1].astype(BF)


def plus(a, b):
    return a[0] + b[0], a[1] + b[1]


def times(rows, right):
    weights = jnp.concatenate(
        [wide(right), jnp.concatenate([-right[1], right[0]], axis=1)], axis=0
    )
    return jnp.dot(rows, weights, preferred_element_type=F32)


def times_transpose(rows, right):
    weights = jnp.concatenate(
        [
            jnp.concatenate([right[0], -right[1]], axis=1),
            jnp.concatenate([right[1], right[0]], axis=1),
        ],
        axis=0,
    )
    return lax.dot_general(rows, weights, (((1,), (1,)), ((), ())), preferred_element_type=F32)


def product(a, b):
    return low(halves(times(wide(a), b)))


def sandwich(factor, middle):
    inner = times(wide(factor), low(middle)).astype(BF)
    return halves(times_transpose(inner, factor))


def get(ref, *index):
    return ref[(*index, 0)], ref[(*index, 1)]


def put(ref, value, *index):
    ref[(*index, 0)] = value[0].astype(ref.dtype)
    ref[(*index, 1)] = value[1].astype(ref.dtype)


def kernel(
    rounds,
    green,
    link,
    lead,
    sigma,
    out,
    own,
    pair,
    board,
    factors,
    base,
    enter,
    onward,
    ends,
    send_sem,
    recv_sem,
):
    layers, width = green.shape[1], green.shape[2]
    energy, me = lax.axis_index("energy"), lax.axis_index("slab")
    role, chip = me % 2, me // 2
    mate = me + 1 - 2 * role
    bits = [(chip // 2**r) % 2 for r in range(rounds)]
    peers = [me + (1 - 2 * bits[r]) * 2 ** (r + 1) for r in range(rounds)]
    sides = [(bits[r] + role) % 2 for r in range(rounds)]

    barrier = pltpu.get_barrier_semaphore()
    for other in [mate] + peers:
        pl.semaphore_signal(barrier, inc=1, device_id=(energy, other), device_id_type=MESH)
    pl.semaphore_wait(barrier, rounds + 1)

    def remote(source, target, other, k):
        return pltpu.make_async_remote_copy(
            src_ref=source,
            dst_ref=target,
            send_sem=send_sem.at[k],
            recv_sem=recv_sem.at[k],
            device_id=(energy, other),
            device_id_type=MESH,
        )

    g = [(green[0, i], green[1, i]) for i in range(layers)]
    c = [(link[0, i], link[1, i]) for i in range(layers)]
    ahead = [low(halves(times_transpose(wide(g[i]), c[i]))) for i in range(layers)]
    back = [product(c[i], g[i]) for i in range(layers)]
    hop = [halves(times_transpose(wide(back[i]), c[i])) for i in range(layers)]

    m_up, s_up = [ahead[0]], [g[0]]
    m_down, s_down = [back[-1]], [hop[-1]]
    for i in range(1, layers):
        s_up.append(plus(sandwich(ahead[i], s_up[-1]), g[i]))
        m_up.append(product(ahead[i], m_up[-1]))
        j = layers - 1 - i
        s_down.insert(0, plus(sandwich(back[j], s_down[0]), hop[j]))
        m_down.insert(0, product(back[j], m_down[0]))

    put(own, m_up[-1], role, 0)
    put(own, s_up[-1], role, 1)
    put(own, m_down[0], 1 - role, 0)
    put(own, s_down[0], 1 - role, 1)
    copy = remote(own.at[1], pair, mate, 0)
    copy.start()

    for i in range(layers):
        put(factors, m_up[i], role, i)
        if i + 1 < layers:
            put(factors, product(g[i], m_down[i + 1]), 1 - role, i)
            put(base, plus(s_up[i], sandwich(g[i], s_down[i + 1])), i)
        else:
            put(factors, g[i], 1 - role, i)
            put(base, s_up[i], i)

    copy.wait()

    def merged(m_first, s_first, m_second, s_second):
        return (
            product(m_second, m_first),
            plus(sandwich(m_second, s_first), s_second),
        )

    total = merged(get(own, 0, 0), get(own, 0, 1), get(pair, 0), get(pair, 1))
    forward = role == 0
    start = (
        jnp.where(forward, lead[0], sigma[0]),
        jnp.where(forward, lead[1], sigma[1]),
    )
    row = lax.broadcasted_iota(jnp.int32, (width, width), 0)
    column = lax.broadcasted_iota(jnp.int32, (width, width), 1)
    square = jnp.where(row == column, 1.0, 0.0).astype(F32)
    nothing = jnp.zeros((width, width), F32)
    m_before, s_before = (square.astype(BF), nothing.astype(BF)), (nothing, nothing)

    def pick(side, a, b):
        return jnp.where(side == 1, a[0], b[0]), jnp.where(side == 1, a[1], b[1])

    pending = None
    for r in range(rounds - 1):
        put(board, total[0], r, sides[r], 0)
        put(board, total[1], r, sides[r], 1)
        copy = remote(board.at[r, sides[r]], board.at[r, sides[r]], peers[r], 1 + r)
        copy.start()
        if pending is not None:
            m_before, s_before = pending()
        copy.wait()
        first, second = (get(board, r, 0, 0), get(board, r, 0, 1)), (get(board, r, 1, 0), get(board, r, 1, 1))
        total = merged(*first, *second)

        def pending(r=r, first=first, m_old=m_before, s_old=s_before):
            if r == 0:
                return (
                    pick(sides[0], first[0], m_old),
                    pick(sides[0], (first[1][0].astype(F32), first[1][1].astype(F32)), s_old),
                )
            m_new, s_new = merged(*first, m_old, s_old)
            return pick(sides[r], m_new, m_old), pick(sides[r], s_new, s_old)

    last = rounds - 1
    put(onward, plus(sandwich(total[0], start), total[1]))
    copy = remote(onward, enter, peers[last], rounds)

    @pl.when(sides[last] == 0)
    def _():
        copy.start()
        put(enter, start)

    if pending is not None:
        m_before, s_before = pending()

    @pl.when(sides[last] == 1)
    def _():
        copy.wait_recv()

    entering = plus(sandwich(m_before, get(enter)), s_before)
    put(ends, entering, role)
    put(pair, plus(sandwich(get(own, 0, 0), entering), get(own, 0, 1)), 0)
    share = remote(pair.at[0], ends.at[role], mate, rounds + 1)
    share.start()

    def spread(k, middle):
        rows = jnp.concatenate([wide(get(factors, k, i)) for i in range(layers)], axis=0)
        inner = times(rows, low(middle)).astype(BF)
        return [
            halves(times_transpose(inner[i * width : (i + 1) * width], get(factors, k, i)))
            for i in range(layers)
        ]

    mine = spread(0, entering)
    for i in range(layers):
        put(base, plus(get(base, i), mine[i]), i)
    share.wait()
    theirs = spread(1, get(ends, 1 - role))
    for i in range(layers):
        value = plus(get(base, i), theirs[i])
        out[0, i] = value[0]
        out[1, i] = value[1]

    @pl.when(sides[last] == 0)
    def _():
        copy.wait_send()


def solution(mesh):
    peers = mesh.shape["slab"]
    rounds = (peers // 2).bit_length() - 1

    def local(slab_green, coupling, left_lead_surface, sigma_right):
        layers, width = slab_green.shape[1], slab_green.shape[2]
        vmem = pl.BlockSpec(memory_space=pltpu.VMEM)
        block = (2, width, width)
        return pl.pallas_call(
            functools.partial(kernel, rounds),
            out_shape=jax.ShapeDtypeStruct(slab_green.shape, F32),
            in_specs=[vmem] * 4,
            out_specs=vmem,
            scratch_shapes=[
                pltpu.VMEM((2, 2, *block), BF),
                pltpu.VMEM((2, *block), BF),
                pltpu.VMEM((max(rounds - 1, 1), 2, 2, *block), BF),
                pltpu.VMEM((2, layers, *block), BF),
                pltpu.VMEM((layers, *block), F32),
                pltpu.VMEM(block, BF),
                pltpu.VMEM(block, BF),
                pltpu.VMEM((2, *block), BF),
                pltpu.SemaphoreType.DMA((rounds + 2,)),
                pltpu.SemaphoreType.DMA((rounds + 2,)),
            ],
            compiler_params=pltpu.CompilerParams(collective_id=0, has_side_effects=True),
        )(slab_green, coupling, left_lead_surface, sigma_right)

    in_specs = (
        P(None, ("energy", "slab"), None, None),
        P(None, ("energy", "slab"), None, None),
        P("energy", None, None),
        P("energy", None, None),
    )
    out_specs = P(None, ("energy", "slab"), None, None)
    return jax.shard_map(local, mesh=mesh, in_specs=in_specs, out_specs=out_specs, check_vma=False)
```

```python
import functools

import jax
import jax.numpy as jnp
from jax import lax
from jax.experimental import pallas as pl
from jax.experimental.pallas import tpu as pltpu
from jax.sharding import PartitionSpec as P

MESH = pl.DeviceIdType.MESH
BF = jnp.bfloat16
F32 = jnp.float32


def wide(value):
    return jnp.concatenate([value[0], value[1]], axis=1)


def halves(out):
    width = out.shape[1] // 2
    return out[:, :width], out[:, width:]


def low(value):
    return value[0].astype(BF), value[1].astype(BF)


def plus(a, b):
    return a[0] + b[0], a[1] + b[1]


def times(rows, right):
    weights = jnp.concatenate(
        [wide(right), jnp.concatenate([-right[1], right[0]], axis=1)], axis=0
    )
    return jnp.dot(rows, weights, preferred_element_type=F32)


def times_transpose(rows, right):
    weights = jnp.concatenate(
        [
            jnp.concatenate([right[0], -right[1]], axis=1),
            jnp.concatenate([right[1], right[0]], axis=1),
        ],
        axis=0,
    )
    return lax.dot_general(rows, weights, (((1,), (1,)), ((), ())), preferred_element_type=F32)


def product(a, b):
    return low(halves(times(wide(a), b)))


def sandwich(factor, middle):
    inner = times(wide(factor), low(middle)).astype(BF)
    return halves(times_transpose(inner, factor))


def get(ref, *index):
    return ref[(*index, 0)], ref[(*index, 1)]


def put(ref, value, *index):
    ref[(*index, 0)] = value[0].astype(ref.dtype)
    ref[(*index, 1)] = value[1].astype(ref.dtype)


def kernel(
    rounds,
    green,
    link,
    lead,
    sigma,
    out,
    own,
    pair,
    board,
    factors,
    base,
    enter,
    onward,
    ends,
    send_sem,
    recv_sem,
):
    layers, width = green.shape[1], green.shape[2]
    energy, me = lax.axis_index("energy"), lax.axis_index("slab")
    role, chip = me % 2, me // 2
    mate = me + 1 - 2 * role
    bits = [(chip // 2**r) % 2 for r in range(rounds)]
    peers = [me + (1 - 2 * bits[r]) * 2 ** (r + 1) for r in range(rounds)]
    sides = [(bits[r] + role) % 2 for r in range(rounds)]

    barrier = pltpu.get_barrier_semaphore()
    for other in [mate] + peers:
        pl.semaphore_signal(barrier, inc=1, device_id=(energy, other), device_id_type=MESH)

    def remote(source, target, other, k):
        return pltpu.make_async_remote_copy(
            src_ref=source,
            dst_ref=target,
            send_sem=send_sem.at[k],
            recv_sem=recv_sem.at[k],
            device_id=(energy, other),
            device_id_type=MESH,
        )

    g = [(green[0, i], green[1, i]) for i in range(layers)]
    c = [(link[0, i], link[1, i]) for i in range(layers)]
    ahead = [low(halves(times_transpose(wide(g[i]), c[i]))) for i in range(layers)]
    back = [product(c[i], g[i]) for i in range(layers)]
    hop = [halves(times_transpose(wide(back[i]), c[i])) for i in range(layers)]

    def merged(first, second):
        return (
            product(second[0], first[0]),
            plus(sandwich(second[0], first[1]), second[1]),
        )

    def whole(items):
        while len(items) > 1:
            rest = items[len(items) // 2 * 2 :]
            items = [merged(*items[k : k + 2]) for k in range(0, len(items) - 1, 2)] + rest
        return items[0]

    up = [(ahead[i], g[i]) for i in range(layers)]
    down = [(back[i], hop[i]) for i in reversed(range(layers))]
    up_total, down_total = whole(up), whole(down)

    put(own, up_total[0], role, 0)
    put(own, up_total[1], role, 1)
    put(own, down_total[0], 1 - role, 0)
    put(own, down_total[1], 1 - role, 1)
    pl.semaphore_wait(barrier, rounds + 1)
    copy = remote(own.at[1], pair, mate, 0)
    copy.start()

    up_part, down_part = [up[0]], [down[0]]
    for i in range(1, layers):
        up_part.append(merged(up_part[-1], up[i]) if i + 1 < layers else up_total)
        if i + 1 < layers:
            down_part.append(merged(down_part[-1], down[i]))
    for i in range(layers):
        m_part, s_part = up_part[i]
        put(factors, m_part, role, i)
        if i + 1 < layers:
            m_rest, s_rest = down_part[layers - 2 - i]
            put(factors, product(g[i], m_rest), 1 - role, i)
            put(base, plus(s_part, sandwich(g[i], s_rest)), i)
        else:
            put(factors, g[i], 1 - role, i)
            put(base, s_part, i)

    copy.wait()

    total = merged((get(own, 0, 0), get(own, 0, 1)), (get(pair, 0), get(pair, 1)))
    forward = role == 0
    start = (
        jnp.where(forward, lead[0], sigma[0]),
        jnp.where(forward, lead[1], sigma[1]),
    )
    row = lax.broadcasted_iota(jnp.int32, (width, width), 0)
    column = lax.broadcasted_iota(jnp.int32, (width, width), 1)
    square = jnp.where(row == column, 1.0, 0.0).astype(F32)
    nothing = jnp.zeros((width, width), F32)
    m_before, s_before = (square.astype(BF), nothing.astype(BF)), (nothing, nothing)

    def pick(side, a, b):
        return jnp.where(side == 1, a[0], b[0]), jnp.where(side == 1, a[1], b[1])

    pending = None
    for r in range(rounds - 1):
        put(board, total[0], r, sides[r], 0)
        put(board, total[1], r, sides[r], 1)
        copy = remote(board.at[r, sides[r]], board.at[r, sides[r]], peers[r], 1 + r)
        copy.start()
        if pending is not None:
            m_before, s_before = pending()
        copy.wait()
        first, second = (get(board, r, 0, 0), get(board, r, 0, 1)), (get(board, r, 1, 0), get(board, r, 1, 1))
        total = merged(first, second)

        def pending(r=r, first=first, m_old=m_before, s_old=s_before):
            if r == 0:
                return (
                    pick(sides[0], first[0], m_old),
                    pick(sides[0], (first[1][0].astype(F32), first[1][1].astype(F32)), s_old),
                )
            m_new, s_new = merged(first, (m_old, s_old))
            return pick(sides[r], m_new, m_old), pick(sides[r], s_new, s_old)

    last = rounds - 1
    put(onward, plus(sandwich(total[0], start), total[1]))
    copy = remote(onward, enter, peers[last], rounds)

    @pl.when(sides[last] == 0)
    def _():
        copy.start()
        put(enter, start)

    if pending is not None:
        m_before, s_before = pending()

    @pl.when(sides[last] == 1)
    def _():
        copy.wait_recv()

    entering = plus(sandwich(m_before, get(enter)), s_before)
    put(ends, entering, role)
    put(pair, plus(sandwich(get(own, 0, 0), entering), get(own, 0, 1)), 0)
    share = remote(pair.at[0], ends.at[role], mate, rounds + 1)
    share.start()

    def spread(k, middle):
        rows = jnp.concatenate([wide(get(factors, k, i)) for i in range(layers)], axis=0)
        inner = times(rows, low(middle)).astype(BF)
        return [
            halves(times_transpose(inner[i * width : (i + 1) * width], get(factors, k, i)))
            for i in range(layers)
        ]

    mine = spread(0, entering)
    for i in range(layers):
        put(base, plus(get(base, i), mine[i]), i)
    share.wait()
    theirs = spread(1, get(ends, 1 - role))
    for i in range(layers):
        value = plus(get(base, i), theirs[i])
        out[0, i] = value[0]
        out[1, i] = value[1]

    @pl.when(sides[last] == 0)
    def _():
        copy.wait_send()


def solution(mesh):
    peers = mesh.shape["slab"]
    rounds = (peers // 2).bit_length() - 1

    def local(slab_green, coupling, left_lead_surface, sigma_right):
        layers, width = slab_green.shape[1], slab_green.shape[2]
        vmem = pl.BlockSpec(memory_space=pltpu.VMEM)
        block = (2, width, width)
        return pl.pallas_call(
            functools.partial(kernel, rounds),
            out_shape=jax.ShapeDtypeStruct(slab_green.shape, F32),
            in_specs=[vmem] * 4,
            out_specs=vmem,
            scratch_shapes=[
                pltpu.VMEM((2, 2, *block), BF),
                pltpu.VMEM((2, *block), BF),
                pltpu.VMEM((max(rounds - 1, 1), 2, 2, *block), BF),
                pltpu.VMEM((2, layers, *block), BF),
                pltpu.VMEM((layers, *block), F32),
                pltpu.VMEM(block, BF),
                pltpu.VMEM(block, BF),
                pltpu.VMEM((2, *block), BF),
                pltpu.SemaphoreType.DMA((rounds + 2,)),
                pltpu.SemaphoreType.DMA((rounds + 2,)),
            ],
            compiler_params=pltpu.CompilerParams(collective_id=0, has_side_effects=True, vmem_limit_bytes=16777216),
        )(slab_green, coupling, left_lead_surface, sigma_right)

    in_specs = (
        P(None, ("energy", "slab"), None, None),
        P(None, ("energy", "slab"), None, None),
        P("energy", None, None),
        P("energy", None, None),
    )
    out_specs = P(None, ("energy", "slab"), None, None)
    return jax.shard_map(local, mesh=mesh, in_specs=in_specs, out_specs=out_specs, check_vma=False)
```

```python
import functools

import jax
import jax.numpy as jnp
from jax import lax
from jax.experimental import pallas as pl
from jax.experimental.pallas import tpu as pltpu
from jax.sharding import PartitionSpec as P

MESH = pl.DeviceIdType.MESH
BF = jnp.bfloat16
F32 = jnp.float32


def wide(value):
    return jnp.concatenate([value[0], value[1]], axis=1)


def halves(out):
    width = out.shape[1] // 2
    return out[:, :width], out[:, width:]


def low(value):
    return value[0].astype(BF), value[1].astype(BF)


def plus(a, b):
    return a[0] + b[0], a[1] + b[1]


def times(rows, right):
    weights = jnp.concatenate(
        [wide(right), jnp.concatenate([-right[1], right[0]], axis=1)], axis=0
    )
    return jnp.dot(rows, weights, preferred_element_type=F32)


def times_transpose(rows, right):
    weights = jnp.concatenate(
        [
            jnp.concatenate([right[0], -right[1]], axis=1),
            jnp.concatenate([right[1], right[0]], axis=1),
        ],
        axis=0,
    )
    return lax.dot_general(rows, weights, (((1,), (1,)), ((), ())), preferred_element_type=F32)


def product(a, b):
    return low(halves(times(wide(a), b)))


def sandwich(factor, middle):
    inner = times(wide(factor), low(middle)).astype(BF)
    return halves(times_transpose(inner, factor))


def get(ref, *index):
    return ref[(*index, 0)], ref[(*index, 1)]


def put(ref, value, *index):
    ref[(*index, 0)] = value[0].astype(ref.dtype)
    ref[(*index, 1)] = value[1].astype(ref.dtype)


def kernel(
    rounds,
    green_hbm,
    link_hbm,
    lead_hbm,
    sigma_hbm,
    out,
    green,
    link,
    lead,
    sigma,
    own,
    pair,
    board,
    factors,
    base,
    enter,
    onward,
    ends,
    send_sem,
    recv_sem,
    load_sem,
):
    loads = [
        pltpu.make_async_copy(source, target, load_sem.at[k])
        for k, (source, target) in enumerate(
            [(green_hbm, green), (link_hbm, link), (lead_hbm, lead), (sigma_hbm, sigma)]
        )
    ]
    for load in loads:
        load.start()
    layers, width = green.shape[1], green.shape[2]
    energy, me = lax.axis_index("energy"), lax.axis_index("slab")
    role, chip = me % 2, me // 2
    mate = me + 1 - 2 * role
    bits = [(chip // 2**r) % 2 for r in range(rounds)]
    peers = [me + (1 - 2 * bits[r]) * 2 ** (r + 1) for r in range(rounds)]
    sides = [(bits[r] + role) % 2 for r in range(rounds)]

    barrier = pltpu.get_barrier_semaphore()
    for other in [mate] + peers:
        pl.semaphore_signal(barrier, inc=1, device_id=(energy, other), device_id_type=MESH)

    def remote(source, target, other, k):
        return pltpu.make_async_remote_copy(
            src_ref=source,
            dst_ref=target,
            send_sem=send_sem.at[k],
            recv_sem=recv_sem.at[k],
            device_id=(energy, other),
            device_id_type=MESH,
        )

    for load in loads:
        load.wait()
    g = [(green[0, i], green[1, i]) for i in range(layers)]
    c = [(link[0, i], link[1, i]) for i in range(layers)]
    ahead = [low(halves(times_transpose(wide(g[i]), c[i]))) for i in range(layers)]
    back = [product(c[i], g[i]) for i in range(layers)]
    hop = [halves(times_transpose(wide(back[i]), c[i])) for i in range(layers)]

    def merged(first, second):
        return (
            product(second[0], first[0]),
            plus(sandwich(second[0], first[1]), second[1]),
        )

    def whole(items):
        while len(items) > 1:
            rest = items[len(items) // 2 * 2 :]
            items = [merged(*items[k : k + 2]) for k in range(0, len(items) - 1, 2)] + rest
        return items[0]

    up = [(ahead[i], g[i]) for i in range(layers)]
    down = [(back[i], hop[i]) for i in reversed(range(layers))]
    up_total, down_total = whole(up), whole(down)

    put(own, up_total[0], role, 0)
    put(own, up_total[1], role, 1)
    put(own, down_total[0], 1 - role, 0)
    put(own, down_total[1], 1 - role, 1)
    pl.semaphore_wait(barrier, rounds + 1)
    copy = remote(own.at[1], pair, mate, 0)
    copy.start()

    up_part, down_part = [up[0]], [down[0]]
    for i in range(1, layers):
        up_part.append(merged(up_part[-1], up[i]) if i + 1 < layers else up_total)
        if i + 1 < layers:
            down_part.append(merged(down_part[-1], down[i]))
    for i in range(layers):
        m_part, s_part = up_part[i]
        put(factors, m_part, role, i)
        if i + 1 < layers:
            m_rest, s_rest = down_part[layers - 2 - i]
            put(factors, product(g[i], m_rest), 1 - role, i)
            put(base, plus(s_part, sandwich(g[i], s_rest)), i)
        else:
            put(factors, g[i], 1 - role, i)
            put(base, s_part, i)

    copy.wait()

    total = merged((get(own, 0, 0), get(own, 0, 1)), (get(pair, 0), get(pair, 1)))
    forward = role == 0
    start = (
        jnp.where(forward, lead[0], sigma[0]),
        jnp.where(forward, lead[1], sigma[1]),
    )
    row = lax.broadcasted_iota(jnp.int32, (width, width), 0)
    column = lax.broadcasted_iota(jnp.int32, (width, width), 1)
    square = jnp.where(row == column, 1.0, 0.0).astype(F32)
    nothing = jnp.zeros((width, width), F32)
    m_before, s_before = (square.astype(BF), nothing.astype(BF)), (nothing, nothing)

    def pick(side, a, b):
        return jnp.where(side == 1, a[0], b[0]), jnp.where(side == 1, a[1], b[1])

    pending = None
    for r in range(rounds - 1):
        put(board, total[0], r, sides[r], 0)
        put(board, total[1], r, sides[r], 1)
        copy = remote(board.at[r, sides[r]], board.at[r, sides[r]], peers[r], 1 + r)
        copy.start()
        if pending is not None:
            m_before, s_before = pending()
        copy.wait()
        first, second = (get(board, r, 0, 0), get(board, r, 0, 1)), (get(board, r, 1, 0), get(board, r, 1, 1))
        total = merged(first, second)

        def pending(r=r, first=first, m_old=m_before, s_old=s_before):
            if r == 0:
                return (
                    pick(sides[0], first[0], m_old),
                    pick(sides[0], (first[1][0].astype(F32), first[1][1].astype(F32)), s_old),
                )
            m_new, s_new = merged(first, (m_old, s_old))
            return pick(sides[r], m_new, m_old), pick(sides[r], s_new, s_old)

    last = rounds - 1
    put(onward, plus(sandwich(total[0], start), total[1]))
    copy = remote(onward, enter, peers[last], rounds)

    @pl.when(sides[last] == 0)
    def _():
        copy.start()
        put(enter, start)

    if pending is not None:
        m_before, s_before = pending()

    @pl.when(sides[last] == 1)
    def _():
        copy.wait_recv()

    entering = plus(sandwich(m_before, get(enter)), s_before)
    put(ends, entering, role)
    put(pair, plus(sandwich(get(own, 0, 0), entering), get(own, 0, 1)), 0)
    share = remote(pair.at[0], ends.at[role], mate, rounds + 1)
    share.start()

    def spread(k, middle):
        rows = jnp.concatenate([wide(get(factors, k, i)) for i in range(layers)], axis=0)
        inner = times(rows, low(middle)).astype(BF)
        return [
            halves(times_transpose(inner[i * width : (i + 1) * width], get(factors, k, i)))
            for i in range(layers)
        ]

    mine = spread(0, entering)
    for i in range(layers):
        put(base, plus(get(base, i), mine[i]), i)
    share.wait()
    theirs = spread(1, get(ends, 1 - role))
    for i in range(layers):
        value = plus(get(base, i), theirs[i])
        out[0, i] = value[0]
        out[1, i] = value[1]

    @pl.when(sides[last] == 0)
    def _():
        copy.wait_send()


def solution(mesh):
    peers = mesh.shape["slab"]
    rounds = (peers // 2).bit_length() - 1

    def local(slab_green, coupling, left_lead_surface, sigma_right):
        layers, width = slab_green.shape[1], slab_green.shape[2]
        vmem = pl.BlockSpec(memory_space=pltpu.VMEM)
        block = (2, width, width)
        return pl.pallas_call(
            functools.partial(kernel, rounds),
            out_shape=jax.ShapeDtypeStruct(slab_green.shape, F32),
            in_specs=[pl.BlockSpec(memory_space=pltpu.HBM)] * 4,
            out_specs=vmem,
            scratch_shapes=[
                pltpu.VMEM(slab_green.shape, BF),
                pltpu.VMEM(coupling.shape, BF),
                pltpu.VMEM(block, BF),
                pltpu.VMEM(block, BF),
                pltpu.VMEM((2, 2, *block), BF),
                pltpu.VMEM((2, *block), BF),
                pltpu.VMEM((max(rounds - 1, 1), 2, 2, *block), BF),
                pltpu.VMEM((2, layers, *block), BF),
                pltpu.VMEM((layers, *block), F32),
                pltpu.VMEM(block, BF),
                pltpu.VMEM(block, BF),
                pltpu.VMEM((2, *block), BF),
                pltpu.SemaphoreType.DMA((rounds + 2,)),
                pltpu.SemaphoreType.DMA((rounds + 2,)),
                pltpu.SemaphoreType.DMA((4,)),
            ],
            compiler_params=pltpu.CompilerParams(collective_id=0, has_side_effects=True, vmem_limit_bytes=16777216),
        )(slab_green, coupling, left_lead_surface, sigma_right)

    in_specs = (
        P(None, ("energy", "slab"), None, None),
        P(None, ("energy", "slab"), None, None),
        P("energy", None, None),
        P("energy", None, None),
    )
    out_specs = P(None, ("energy", "slab"), None, None)
    return jax.shard_map(local, mesh=mesh, in_specs=in_specs, out_specs=out_specs, check_vma=False)
```

```python
import functools

import jax
import jax.numpy as jnp
from jax import lax
from jax.experimental import pallas as pl
from jax.experimental.pallas import tpu as pltpu
from jax.sharding import PartitionSpec as P

MESH = pl.DeviceIdType.MESH
BF = jnp.bfloat16
F32 = jnp.float32


def wide(value):
    return jnp.concatenate([value[0], value[1]], axis=1)


def halves(out):
    width = out.shape[1] // 2
    return out[:, :width], out[:, width:]


def low(value):
    return value[0].astype(BF), value[1].astype(BF)


def plus(a, b):
    return a[0] + b[0], a[1] + b[1]


def times(rows, right):
    weights = jnp.concatenate(
        [wide(right), jnp.concatenate([-right[1], right[0]], axis=1)], axis=0
    )
    return jnp.dot(rows, weights, preferred_element_type=F32)


def times_transpose(rows, right):
    weights = jnp.concatenate(
        [
            jnp.concatenate([right[0], -right[1]], axis=1),
            jnp.concatenate([right[1], right[0]], axis=1),
        ],
        axis=0,
    )
    return lax.dot_general(rows, weights, (((1,), (1,)), ((), ())), preferred_element_type=F32)


def product(a, b):
    return low(halves(times(wide(a), b)))


def sandwich(factor, middle):
    inner = times(wide(factor), low(middle)).astype(BF)
    return halves(times_transpose(inner, factor))


def get(ref, *index):
    return ref[(*index, 0)], ref[(*index, 1)]


def put(ref, value, *index):
    ref[(*index, 0)] = value[0].astype(ref.dtype)
    ref[(*index, 1)] = value[1].astype(ref.dtype)


def kernel(
    rounds,
    green_hbm,
    link_hbm,
    lead_hbm,
    sigma_hbm,
    out,
    green,
    link,
    lead,
    sigma,
    own,
    pair,
    board,
    factors,
    base,
    enter,
    onward,
    ends,
    send_sem,
    recv_sem,
    load_sem,
):
    loads = [
        pltpu.make_async_copy(source, target, load_sem.at[k])
        for k, (source, target) in enumerate(
            [(green_hbm, green), (link_hbm, link), (lead_hbm, lead), (sigma_hbm, sigma)]
        )
    ]
    for load in loads:
        load.start()
    layers, width = green.shape[1], green.shape[2]
    energy, me = lax.axis_index("energy"), lax.axis_index("slab")
    role, chip = me % 2, me // 2
    mate = me + 1 - 2 * role
    bits = [(chip // 2**r) % 2 for r in range(rounds)]
    peers = [me + (1 - 2 * bits[r]) * 2 ** (r + 1) for r in range(rounds)]
    sides = [(bits[r] + role) % 2 for r in range(rounds)]

    barrier = pltpu.get_barrier_semaphore()
    for other in [mate] + peers:
        pl.semaphore_signal(barrier, inc=1, device_id=(energy, other), device_id_type=MESH)

    def remote(source, target, other, k):
        return pltpu.make_async_remote_copy(
            src_ref=source,
            dst_ref=target,
            send_sem=send_sem.at[k],
            recv_sem=recv_sem.at[k],
            device_id=(energy, other),
            device_id_type=MESH,
        )

    for load in loads:
        load.wait()
    g = [(green[0, i], green[1, i]) for i in range(layers)]
    c = [(link[0, i], link[1, i]) for i in range(layers)]
    ahead = [low(halves(times_transpose(wide(g[i]), c[i]))) for i in range(layers)]
    back = [product(c[i], g[i]) for i in range(layers)]
    hop = [halves(times_transpose(wide(back[i]), c[i])) for i in range(layers)]

    def merged(first, second):
        return (
            product(second[0], first[0]),
            plus(sandwich(second[0], first[1]), second[1]),
        )

    def whole(items):
        while len(items) > 1:
            rest = items[len(items) // 2 * 2 :]
            items = [merged(*items[k : k + 2]) for k in range(0, len(items) - 1, 2)] + rest
        return items[0]

    up = [(ahead[i], g[i]) for i in range(layers)]
    down = [(back[i], hop[i]) for i in reversed(range(layers))]
    up_total, down_total = whole(up), whole(down)

    put(own, up_total[0], role, 0)
    put(own, up_total[1], role, 1)
    put(own, down_total[0], 1 - role, 0)
    put(own, down_total[1], 1 - role, 1)
    pl.semaphore_wait(barrier, rounds + 1)
    copy = remote(own.at[1], pair, mate, 0)
    copy.start()

    up_part, down_part = [up[0]], [down[0]]
    for i in range(1, layers):
        up_part.append(merged(up_part[-1], up[i]) if i + 1 < layers else up_total)
        if i + 1 < layers:
            down_part.append(merged(down_part[-1], down[i]))
    for i in range(layers):
        m_part, s_part = up_part[i]
        put(factors, m_part, role, i)
        if i + 1 < layers:
            m_rest, s_rest = down_part[layers - 2 - i]
            put(factors, product(g[i], m_rest), 1 - role, i)
            put(base, plus(s_part, sandwich(g[i], s_rest)), i)
        else:
            put(factors, g[i], 1 - role, i)
            put(base, s_part, i)

    copy.wait()

    total = merged((get(own, 0, 0), get(own, 0, 1)), (get(pair, 0), get(pair, 1)))
    forward = role == 0
    start = (
        jnp.where(forward, lead[0], sigma[0]),
        jnp.where(forward, lead[1], sigma[1]),
    )
    row = lax.broadcasted_iota(jnp.int32, (width, width), 0)
    column = lax.broadcasted_iota(jnp.int32, (width, width), 1)
    square = jnp.where(row == column, 1.0, 0.0).astype(F32)
    nothing = jnp.zeros((width, width), F32)
    m_before, s_before = (square.astype(BF), nothing.astype(BF)), (nothing, nothing)

    def pick(side, a, b):
        return jnp.where(side == 1, a[0], b[0]), jnp.where(side == 1, a[1], b[1])

    pending = None
    for r in range(rounds - 1):
        put(board, total[0], r, sides[r], 0)
        put(board, total[1], r, sides[r], 1)
        copy = remote(board.at[r, sides[r]], board.at[r, sides[r]], peers[r], 1 + r)
        copy.start()
        if pending is not None:
            m_before, s_before = pending()
        copy.wait()
        first, second = (get(board, r, 0, 0), get(board, r, 0, 1)), (get(board, r, 1, 0), get(board, r, 1, 1))
        total = merged(first, second)

        def pending(r=r, first=first, m_old=m_before, s_old=s_before):
            if r == 0:
                return (
                    pick(sides[0], first[0], m_old),
                    pick(sides[0], (first[1][0].astype(F32), first[1][1].astype(F32)), s_old),
                )
            m_new, s_new = merged(first, (m_old, s_old))
            return pick(sides[r], m_new, m_old), pick(sides[r], s_new, s_old)

    last = rounds - 1
    put(onward, plus(sandwich(total[0], start), total[1]))
    copy = remote(onward, enter, peers[last], rounds)

    @pl.when(sides[last] == 0)
    def _():
        copy.start()
        put(enter, start)

    if pending is not None:
        m_before, s_before = pending()

    @pl.when(sides[last] == 1)
    def _():
        copy.wait_recv()

    entering = plus(sandwich(m_before, get(enter)), s_before)
    put(ends, entering, role)
    put(pair, plus(sandwich(get(own, 0, 0), entering), get(own, 0, 1)), 0)
    share = remote(pair.at[0], ends.at[role], mate, rounds + 1)
    share.start()

    def spread(k, middle):
        rows = jnp.concatenate([wide(get(factors, k, i)) for i in range(layers)], axis=0)
        inner = times(rows, low(middle)).astype(BF)
        return [
            halves(times_transpose(inner[i * width : (i + 1) * width], get(factors, k, i)))
            for i in range(layers)
        ]

    mine = spread(0, entering)
    for i in range(layers):
        put(base, plus(get(base, i), mine[i]), i)
    share.wait()
    theirs = spread(1, get(ends, 1 - role))
    for i in range(layers):
        value = plus(get(base, i), theirs[i])
        out[0, i] = value[0]
        out[1, i] = value[1]

    @pl.when(sides[last] == 0)
    def _():
        copy.wait_send()


def solution(mesh):
    peers = mesh.shape["slab"]
    rounds = (peers // 2).bit_length() - 1

    def local(slab_green, coupling, left_lead_surface, sigma_right):
        layers, width = slab_green.shape[1], slab_green.shape[2]
        vmem = pl.BlockSpec(memory_space=pltpu.VMEM)
        block = (2, width, width)
        return pl.pallas_call(
            functools.partial(kernel, rounds),
            out_shape=jax.ShapeDtypeStruct(slab_green.shape, F32),
            in_specs=[pl.BlockSpec(memory_space=pltpu.HBM)] * 4,
            out_specs=vmem,
            scratch_shapes=[
                pltpu.VMEM(slab_green.shape, BF),
                pltpu.VMEM(coupling.shape, BF),
                pltpu.VMEM(block, BF),
                pltpu.VMEM(block, BF),
                pltpu.VMEM((2, 2, *block), BF),
                pltpu.VMEM((2, *block), BF),
                pltpu.VMEM((max(rounds - 1, 1), 2, 2, *block), BF),
                pltpu.VMEM((2, layers, *block), BF),
                pltpu.VMEM((layers, *block), F32),
                pltpu.VMEM(block, BF),
                pltpu.VMEM(block, BF),
                pltpu.VMEM((2, *block), BF),
                pltpu.SemaphoreType.DMA((rounds + 2,)),
                pltpu.SemaphoreType.DMA((rounds + 2,)),
                pltpu.SemaphoreType.DMA((4,)),
            ],
            compiler_params=pltpu.CompilerParams(collective_id=0, has_side_effects=True, vmem_limit_bytes=16777216),
        )(*[pltpu.with_memory_space_constraint(a, pltpu.HBM) for a in (slab_green, coupling, left_lead_surface, sigma_right)])

    in_specs = (
        P(None, ("energy", "slab"), None, None),
        P(None, ("energy", "slab"), None, None),
        P("energy", None, None),
        P("energy", None, None),
    )
    out_specs = P(None, ("energy", "slab"), None, None)
    return jax.shard_map(local, mesh=mesh, in_specs=in_specs, out_specs=out_specs, check_vma=False)
```

```python
import functools

import jax
import jax.numpy as jnp
from jax import lax
from jax.experimental import pallas as pl
from jax.experimental.pallas import tpu as pltpu
from jax.sharding import PartitionSpec as P

MESH = pl.DeviceIdType.MESH
BF = jnp.bfloat16
F32 = jnp.float32


def wide(value):
    return jnp.concatenate([value[0], value[1]], axis=1)


def halves(out):
    width = out.shape[1] // 2
    return out[:, :width], out[:, width:]


def low(value):
    return value[0].astype(BF), value[1].astype(BF)


def plus(a, b):
    return a[0] + b[0], a[1] + b[1]


def times(rows, right):
    weights = jnp.concatenate(
        [wide(right), jnp.concatenate([-right[1], right[0]], axis=1)], axis=0
    )
    return jnp.dot(rows, weights, preferred_element_type=F32)


def times_transpose(rows, right):
    weights = jnp.concatenate(
        [
            jnp.concatenate([right[0], -right[1]], axis=1),
            jnp.concatenate([right[1], right[0]], axis=1),
        ],
        axis=0,
    )
    return lax.dot_general(rows, weights, (((1,), (1,)), ((), ())), preferred_element_type=F32)


def product(a, b):
    return low(halves(times(wide(a), b)))


def sandwich(factor, middle):
    inner = times(wide(factor), low(middle)).astype(BF)
    return halves(times_transpose(inner, factor))


def get(ref, *index):
    return ref[(*index, 0)], ref[(*index, 1)]


def put(ref, value, *index):
    ref[(*index, 0)] = value[0].astype(ref.dtype)
    ref[(*index, 1)] = value[1].astype(ref.dtype)


def kernel(
    rounds,
    green_hbm,
    link_hbm,
    lead_hbm,
    sigma_hbm,
    out,
    green,
    link,
    lead,
    sigma,
    own,
    pair,
    board,
    factors,
    base,
    inbox,
    outbox,
    ends,
    send_sem,
    recv_sem,
    load_sem,
):
    loads = [
        pltpu.make_async_copy(source, target, load_sem.at[k])
        for k, (source, target) in enumerate(
            [(green_hbm, green), (link_hbm, link), (lead_hbm, lead), (sigma_hbm, sigma)]
        )
    ]
    for load in loads:
        load.start()
    layers, width = green.shape[1], green.shape[2]
    energy, me = lax.axis_index("energy"), lax.axis_index("slab")
    role, chip = me % 2, me // 2
    mate = me + 1 - 2 * role
    bit = chip % 2
    side = (bit + role) % 2
    pal = me + (1 - 2 * bit) * 2
    steps = rounds - 1
    spot = chip // 2
    place = spot + role * (2**steps - 1 - 2 * spot)
    stride = (1 - 2 * role) * 4
    lows = [place // 2 ** (k + 1) * 2 ** (k + 1) for k in range(steps)]
    gives = [place == lows[k] + 2**k - 1 for k in range(steps)]
    takes = [(place // 2**k) % 2 == 1 for k in range(steps)]
    givers = [me + stride * (lows[k] + 2**k - 1 - place) for k in range(steps)]

    barrier = pltpu.get_barrier_semaphore()

    def greet(other):
        pl.semaphore_signal(barrier, inc=1, device_id=(energy, other), device_id_type=MESH)

    expected = 2
    greet(mate)
    greet(pal)
    for k in range(steps):
        expected = expected + jnp.where(gives[k], 2**k, 0) + jnp.where(takes[k], 1, 0)

        @pl.when(gives[k])
        def _():
            for d in range(2**k):
                greet(me + stride * (1 + d))

        @pl.when(takes[k])
        def _():
            greet(givers[k])

    def remote(source, target, other, sender, receiver):
        return pltpu.make_async_remote_copy(
            src_ref=source,
            dst_ref=target,
            send_sem=send_sem.at[sender],
            recv_sem=recv_sem.at[receiver],
            device_id=(energy, other),
            device_id_type=MESH,
        )

    zeros = jnp.zeros((width, width), BF)
    for k in range(steps):

        @pl.when(jnp.logical_not(takes[k]))
        def _():
            put(inbox, (zeros, zeros), k, 1)

        @pl.when(jnp.logical_or(jnp.logical_not(takes[k]), lows[k] == 0))
        def _():
            put(inbox, (zeros, zeros), k, 0)

    for load in loads:
        load.wait()
    g = [(green[0, i], green[1, i]) for i in range(layers)]
    c = [(link[0, i], link[1, i]) for i in range(layers)]
    ahead = [low(halves(times_transpose(wide(g[i]), c[i]))) for i in range(layers)]
    back = [product(c[i], g[i]) for i in range(layers)]
    hop = [halves(times_transpose(wide(back[i]), c[i])) for i in range(layers)]

    def merged(first, second):
        return (
            product(second[0], first[0]),
            plus(sandwich(second[0], first[1]), second[1]),
        )

    def whole(items):
        while len(items) > 1:
            rest = items[len(items) // 2 * 2 :]
            items = [merged(*items[k : k + 2]) for k in range(0, len(items) - 1, 2)] + rest
        return items[0]

    up = [(ahead[i], g[i]) for i in range(layers)]
    down = [(back[i], hop[i]) for i in reversed(range(layers))]
    up_total, down_total = whole(up), whole(down)

    put(own, up_total[0], role, 0)
    put(own, up_total[1], role, 1)
    put(own, down_total[0], 1 - role, 0)
    put(own, down_total[1], 1 - role, 1)
    pl.semaphore_wait(barrier, expected)
    swap = remote(own.at[1], pair, mate, 0, 0)
    swap.start()

    up_part, down_part = [up[0]], [down[0]]
    for i in range(1, layers):
        up_part.append(merged(up_part[-1], up[i]) if i + 1 < layers else up_total)
        if i + 1 < layers:
            down_part.append(merged(down_part[-1], down[i]))
    for i in range(layers):
        m_part, s_part = up_part[i]
        put(factors, m_part, role, i)
        if i + 1 < layers:
            m_rest, s_rest = down_part[layers - 2 - i]
            put(factors, product(g[i], m_rest), 1 - role, i)
            put(base, plus(s_part, sandwich(g[i], s_rest)), i)
        else:
            put(factors, g[i], 1 - role, i)
            put(base, s_part, i)

    swap.wait_recv()
    total = merged((get(own, 0, 0), get(own, 0, 1)), (get(pair, 0), get(pair, 1)))
    forward = role == 0
    start = (
        jnp.where(forward, lead[0], sigma[0]),
        jnp.where(forward, lead[1], sigma[1]),
    )
    row = lax.broadcasted_iota(jnp.int32, (width, width), 0)
    column = lax.broadcasted_iota(jnp.int32, (width, width), 1)
    square = jnp.where(row == column, 1.0, 0.0).astype(BF)

    def wider(value):
        return value[0].astype(F32), value[1].astype(F32)

    def pick(test, a, b):
        return jnp.where(test, a[0], b[0]), jnp.where(test, a[1], b[1])

    def choose(test, a, b):
        return pick(test, a[0], b[0]), pick(test, a[1], b[1])

    put(board, total[0], side, 0)
    put(board, total[1], side, 1)
    cross = remote(board.at[side], board.at[side], pal, 1, 1)
    cross.start()
    cross.wait_recv()
    first = (get(board, 0, 0), wider(get(board, 0, 1)))
    second = (get(board, 1, 0), wider(get(board, 1, 1)))
    total = merged(first, second)
    none = (zeros, zeros)
    head = place == 0

    def settled(value):
        return pick(head, none, value[0]), pick(
            head, plus(sandwich(value[0], start), value[1]), value[1]
        )

    total = settled(total)

    def deliveries(k):
        found = []
        for d in range(2**k):
            other = me + stride * (1 + d)
            at = 2 + 2 * (2**k - 1 + d)
            found.append(
                (
                    remote(outbox.at[k, 1], inbox.at[k, 1], other, at, 2 + 2 * k),
                    remote(outbox.at[k, 0], inbox.at[k, 0], other, at + 1, 3 + 2 * k),
                )
            )
        return found

    def send(k):
        @pl.when(gives[k])
        def _():
            put(outbox, total[1], k, 1)
            put(outbox, total[0], k, 0)
            sent = deliveries(k)
            for constant, _ in sent:
                constant.start()
            if k + 1 < steps:

                @pl.when(lows[k] != 0)
                def _():
                    for _, linear in sent:
                        linear.start()

    def receive(k):
        @pl.when(takes[k])
        def _():
            constant, linear = deliveries(k)[0]
            constant.wait_recv()
            if k + 1 < steps:

                @pl.when(lows[k] != 0)
                def _():
                    linear.wait_recv()

        return get(inbox, k, 0), wider(get(inbox, k, 1))

    def finish(k):
        @pl.when(gives[k])
        def _():
            sent = deliveries(k)
            for constant, _ in sent:
                constant.wait_send()
            if k + 1 < steps:

                @pl.when(lows[k] != 0)
                def _():
                    for _, linear in sent:
                        linear.wait_send()

    if steps:
        send(0)
    before = settled(
        (
            pick(side == 1, first[0], (square, zeros)),
            pick(side == 1, first[1], wider(none)),
        )
    )
    for k in range(steps):
        got = receive(k)
        if k + 1 < steps:
            total = choose(takes[k], merged(got, total), total)
            send(k + 1)
        before = choose(takes[k], merged(got, before), before)
    entering = before[1]
    put(ends, entering, role)
    put(pair, plus(sandwich(get(own, 0, 0), entering), get(own, 0, 1)), 0)
    last = 2 + 2 * steps
    share = remote(pair.at[0], ends.at[role], mate, 2 * 2**steps, last)
    share.start()

    def spread(k, middle):
        rows = jnp.concatenate([wide(get(factors, k, i)) for i in range(layers)], axis=0)
        inner = times(rows, low(middle)).astype(BF)
        return [
            halves(times_transpose(inner[i * width : (i + 1) * width], get(factors, k, i)))
            for i in range(layers)
        ]

    mine = spread(0, entering)
    for i in range(layers):
        put(base, plus(get(base, i), mine[i]), i)
    share.wait_recv()
    theirs = spread(1, get(ends, 1 - role))
    for i in range(layers):
        value = plus(get(base, i), theirs[i])
        out[0, i] = value[0]
        out[1, i] = value[1]

    swap.wait_send()
    cross.wait_send()
    share.wait_send()
    for k in range(steps):
        finish(k)


def solution(mesh):
    peers = mesh.shape["slab"]
    rounds = (peers // 2).bit_length() - 1

    def local(slab_green, coupling, left_lead_surface, sigma_right):
        layers, width = slab_green.shape[1], slab_green.shape[2]
        vmem = pl.BlockSpec(memory_space=pltpu.VMEM)
        block = (2, width, width)
        return pl.pallas_call(
            functools.partial(kernel, rounds),
            out_shape=jax.ShapeDtypeStruct(slab_green.shape, F32),
            in_specs=[pl.BlockSpec(memory_space=pltpu.HBM)] * 4,
            out_specs=vmem,
            scratch_shapes=[
                pltpu.VMEM(slab_green.shape, BF),
                pltpu.VMEM(coupling.shape, BF),
                pltpu.VMEM(block, BF),
                pltpu.VMEM(block, BF),
                pltpu.VMEM((2, 2, *block), BF),
                pltpu.VMEM((2, *block), BF),
                pltpu.VMEM((2, 2, *block), BF),
                pltpu.VMEM((2, layers, *block), BF),
                pltpu.VMEM((layers, *block), F32),
                pltpu.VMEM((max(rounds - 1, 1), 2, *block), BF),
                pltpu.VMEM((max(rounds - 1, 1), 2, *block), BF),
                pltpu.VMEM((2, *block), BF),
                pltpu.SemaphoreType.DMA((2**rounds + 1,)),
                pltpu.SemaphoreType.DMA((2 * rounds + 1,)),
                pltpu.SemaphoreType.DMA((4,)),
            ],
            compiler_params=pltpu.CompilerParams(collective_id=0, has_side_effects=True, vmem_limit_bytes=16777216),
        )(*[pltpu.with_memory_space_constraint(a, pltpu.HBM) for a in (slab_green, coupling, left_lead_surface, sigma_right)])

    in_specs = (
        P(None, ("energy", "slab"), None, None),
        P(None, ("energy", "slab"), None, None),
        P("energy", None, None),
        P("energy", None, None),
    )
    out_specs = P(None, ("energy", "slab"), None, None)
    return jax.shard_map(local, mesh=mesh, in_specs=in_specs, out_specs=out_specs, check_vma=False)
```

```python
import functools

import jax
import jax.numpy as jnp
from jax import lax
from jax.experimental import pallas as pl
from jax.experimental.pallas import tpu as pltpu
from jax.sharding import PartitionSpec as P

MESH = pl.DeviceIdType.MESH
BF = jnp.bfloat16
F32 = jnp.float32


def wide(value):
    return jnp.concatenate([value[0], value[1]], axis=1)


def halves(out):
    width = out.shape[1] // 2
    return out[:, :width], out[:, width:]


def low(value):
    return value[0].astype(BF), value[1].astype(BF)


def plus(a, b):
    return a[0] + b[0], a[1] + b[1]


def times(rows, right):
    weights = jnp.concatenate(
        [wide(right), jnp.concatenate([-right[1], right[0]], axis=1)], axis=0
    )
    return jnp.dot(rows, weights, preferred_element_type=F32)


def times_transpose(rows, right):
    weights = jnp.concatenate(
        [
            jnp.concatenate([right[0], -right[1]], axis=1),
            jnp.concatenate([right[1], right[0]], axis=1),
        ],
        axis=0,
    )
    return lax.dot_general(rows, weights, (((1,), (1,)), ((), ())), preferred_element_type=F32)


def product(a, b):
    return low(halves(times(wide(a), b)))


def sandwich(factor, middle):
    inner = times(wide(factor), low(middle)).astype(BF)
    return halves(times_transpose(inner, factor))


def get(ref, *index):
    return ref[(*index, 0)], ref[(*index, 1)]


def put(ref, value, *index):
    ref[(*index, 0)] = value[0].astype(ref.dtype)
    ref[(*index, 1)] = value[1].astype(ref.dtype)


def kernel(
    rounds,
    green_hbm,
    link_hbm,
    lead_hbm,
    sigma_hbm,
    out,
    green,
    link,
    lead,
    sigma,
    own,
    pair,
    given,
    board,
    factors,
    base,
    inbox,
    outbox,
    ends,
    send_sem,
    recv_sem,
    load_sem,
):
    loads = [
        pltpu.make_async_copy(source, target, load_sem.at[k])
        for k, (source, target) in enumerate(
            [(green_hbm, green), (link_hbm, link), (lead_hbm, lead), (sigma_hbm, sigma)]
        )
    ]
    for load in loads:
        load.start()
    layers, width = green.shape[1], green.shape[2]
    energy, me = lax.axis_index("energy"), lax.axis_index("slab")
    role, chip = me % 2, me // 2
    mate = me + 1 - 2 * role
    bit = chip % 2
    side = (bit + role) % 2
    pal = me + (1 - 2 * bit) * 2
    steps = rounds - 1
    spot = chip // 2
    place = spot + role * (2**steps - 1 - 2 * spot)
    stride = (1 - 2 * role) * 4
    lows = [place // 2 ** (k + 1) * 2 ** (k + 1) for k in range(steps)]
    gives = [place == lows[k] + 2**k - 1 for k in range(steps)]
    takes = [(place // 2**k) % 2 == 1 for k in range(steps)]
    givers = [me + stride * (lows[k] + 2**k - 1 - place) for k in range(steps)]

    barrier = pltpu.get_barrier_semaphore()

    def greet(other):
        pl.semaphore_signal(barrier, inc=1, device_id=(energy, other), device_id_type=MESH)

    expected = 2
    greet(mate)
    greet(pal)
    for k in range(steps):
        expected = expected + jnp.where(gives[k], 2**k, 0) + jnp.where(takes[k], 1, 0)

        @pl.when(gives[k])
        def _():
            for d in range(2**k):
                greet(me + stride * (1 + d))

        @pl.when(takes[k])
        def _():
            greet(givers[k])

    def remote(source, target, other, sender, receiver):
        return pltpu.make_async_remote_copy(
            src_ref=source,
            dst_ref=target,
            send_sem=send_sem.at[sender],
            recv_sem=recv_sem.at[receiver],
            device_id=(energy, other),
            device_id_type=MESH,
        )

    zeros = jnp.zeros((width, width), BF)
    for k in range(steps):

        @pl.when(jnp.logical_not(takes[k]))
        def _():
            put(inbox, (zeros, zeros), k, 1)

        @pl.when(jnp.logical_or(jnp.logical_not(takes[k]), lows[k] == 0))
        def _():
            put(inbox, (zeros, zeros), k, 0)

    for load in loads:
        load.wait()
    g = [(green[0, i], green[1, i]) for i in range(layers)]
    c = [(link[0, i], link[1, i]) for i in range(layers)]
    ahead = [low(halves(times_transpose(wide(g[i]), c[i]))) for i in range(layers)]
    back = [product(c[i], g[i]) for i in range(layers)]
    hop = [halves(times_transpose(wide(back[i]), c[i])) for i in range(layers)]

    def merged(first, second):
        return (
            product(second[0], first[0]),
            plus(sandwich(second[0], first[1]), second[1]),
        )

    def whole(items):
        while len(items) > 1:
            rest = items[len(items) // 2 * 2 :]
            items = [merged(*items[k : k + 2]) for k in range(0, len(items) - 1, 2)] + rest
        return items[0]

    up = [(ahead[i], g[i]) for i in range(layers)]
    down = [(back[i], hop[i]) for i in reversed(range(layers))]
    up_total, down_total = whole(up), whole(down)

    put(own, up_total[0], role, 0)
    put(own, up_total[1], role, 1)
    put(own, down_total[0], 1 - role, 0)
    put(own, down_total[1], 1 - role, 1)
    pl.semaphore_wait(barrier, expected)
    swap = remote(own.at[1], pair, mate, 0, 0)
    swap.start()

    up_part, down_part = [up[0]], [down[0]]
    for i in range(1, layers):
        up_part.append(merged(up_part[-1], up[i]) if i + 1 < layers else up_total)
        if i + 1 < layers:
            down_part.append(merged(down_part[-1], down[i]))
    for i in range(layers):
        m_part, s_part = up_part[i]
        put(factors, m_part, role, i)
        if i + 1 < layers:
            m_rest, s_rest = down_part[layers - 2 - i]
            put(factors, product(g[i], m_rest), 1 - role, i)
            put(base, plus(s_part, sandwich(g[i], s_rest)), i)
        else:
            put(factors, g[i], 1 - role, i)
            put(base, s_part, i)

    swap.wait_recv()
    last = 2 + 2 * steps
    hint = remote(own.at[0], given, mate, 2 * 2**steps + 1, last + 1)
    hint.start()
    total = merged((get(own, 0, 0), get(own, 0, 1)), (get(pair, 0), get(pair, 1)))
    forward = role == 0
    start = (
        jnp.where(forward, lead[0], sigma[0]),
        jnp.where(forward, lead[1], sigma[1]),
    )
    row = lax.broadcasted_iota(jnp.int32, (width, width), 0)
    column = lax.broadcasted_iota(jnp.int32, (width, width), 1)
    square = jnp.where(row == column, 1.0, 0.0).astype(BF)

    def wider(value):
        return value[0].astype(F32), value[1].astype(F32)

    def pick(test, a, b):
        return jnp.where(test, a[0], b[0]), jnp.where(test, a[1], b[1])

    def choose(test, a, b):
        return pick(test, a[0], b[0]), pick(test, a[1], b[1])

    put(board, total[0], side, 0)
    put(board, total[1], side, 1)
    cross = remote(board.at[side], board.at[side], pal, 1, 1)
    cross.start()
    cross.wait_recv()
    first = (get(board, 0, 0), wider(get(board, 0, 1)))
    second = (get(board, 1, 0), wider(get(board, 1, 1)))
    total = merged(first, second)
    none = (zeros, zeros)
    head = place == 0

    def settled(value):
        return pick(head, none, value[0]), pick(
            head, plus(sandwich(value[0], start), value[1]), value[1]
        )

    total = settled(total)

    def deliveries(k):
        found = []
        for d in range(2**k):
            other = me + stride * (1 + d)
            at = 2 + 2 * (2**k - 1 + d)
            found.append(
                (
                    remote(outbox.at[k, 1], inbox.at[k, 1], other, at, 2 + 2 * k),
                    remote(outbox.at[k, 0], inbox.at[k, 0], other, at + 1, 3 + 2 * k),
                )
            )
        return found

    def send(k):
        @pl.when(gives[k])
        def _():
            put(outbox, total[1], k, 1)
            put(outbox, total[0], k, 0)
            sent = deliveries(k)
            for constant, _ in sent:
                constant.start()
            if k + 1 < steps:

                @pl.when(lows[k] != 0)
                def _():
                    for _, linear in sent:
                        linear.start()

    def receive(k):
        @pl.when(takes[k])
        def _():
            constant, linear = deliveries(k)[0]
            constant.wait_recv()
            if k + 1 < steps:

                @pl.when(lows[k] != 0)
                def _():
                    linear.wait_recv()

        return get(inbox, k, 0), wider(get(inbox, k, 1))

    def finish(k):
        @pl.when(gives[k])
        def _():
            sent = deliveries(k)
            for constant, _ in sent:
                constant.wait_send()
            if k + 1 < steps:

                @pl.when(lows[k] != 0)
                def _():
                    for _, linear in sent:
                        linear.wait_send()

    if steps:
        send(0)
    before = settled(
        (
            pick(side == 1, first[0], (square, zeros)),
            pick(side == 1, first[1], wider(none)),
        )
    )
    hint.wait_recv()
    for i in range(layers):
        factor = get(factors, 1, i)
        put(base, plus(get(base, i), sandwich(factor, get(given, 1))), i)
        put(factors, product(factor, get(given, 0)), 1, i)
    for k in range(steps):
        got = receive(k)
        if k + 1 < steps:
            total = choose(takes[k], merged(got, total), total)
            send(k + 1)
        before = choose(takes[k], merged(got, before), before)
    entering = before[1]
    put(ends, entering, role)
    share = remote(ends.at[role], ends.at[role], mate, 2 * 2**steps, last)
    share.start()

    def spread(k, middle):
        rows = jnp.concatenate([wide(get(factors, k, i)) for i in range(layers)], axis=0)
        inner = times(rows, low(middle)).astype(BF)
        return [
            halves(times_transpose(inner[i * width : (i + 1) * width], get(factors, k, i)))
            for i in range(layers)
        ]

    mine = spread(0, entering)
    for i in range(layers):
        put(base, plus(get(base, i), mine[i]), i)
    share.wait_recv()
    theirs = spread(1, get(ends, 1 - role))
    for i in range(layers):
        value = plus(get(base, i), theirs[i])
        out[0, i] = value[0]
        out[1, i] = value[1]

    swap.wait_send()
    hint.wait_send()
    cross.wait_send()
    share.wait_send()
    for k in range(steps):
        finish(k)


def solution(mesh):
    peers = mesh.shape["slab"]
    rounds = (peers // 2).bit_length() - 1

    def local(slab_green, coupling, left_lead_surface, sigma_right):
        layers, width = slab_green.shape[1], slab_green.shape[2]
        vmem = pl.BlockSpec(memory_space=pltpu.VMEM)
        block = (2, width, width)
        return pl.pallas_call(
            functools.partial(kernel, rounds),
            out_shape=jax.ShapeDtypeStruct(slab_green.shape, F32),
            in_specs=[pl.BlockSpec(memory_space=pltpu.HBM)] * 4,
            out_specs=vmem,
            scratch_shapes=[
                pltpu.VMEM(slab_green.shape, BF),
                pltpu.VMEM(coupling.shape, BF),
                pltpu.VMEM(block, BF),
                pltpu.VMEM(block, BF),
                pltpu.VMEM((2, 2, *block), BF),
                pltpu.VMEM((2, *block), BF),
                pltpu.VMEM((2, *block), BF),
                pltpu.VMEM((2, 2, *block), BF),
                pltpu.VMEM((2, layers, *block), BF),
                pltpu.VMEM((layers, *block), F32),
                pltpu.VMEM((max(rounds - 1, 1), 2, *block), BF),
                pltpu.VMEM((max(rounds - 1, 1), 2, *block), BF),
                pltpu.VMEM((2, *block), BF),
                pltpu.SemaphoreType.DMA((2**rounds + 2,)),
                pltpu.SemaphoreType.DMA((2 * rounds + 2,)),
                pltpu.SemaphoreType.DMA((4,)),
            ],
            compiler_params=pltpu.CompilerParams(collective_id=0, has_side_effects=True, vmem_limit_bytes=16777216),
        )(*[pltpu.with_memory_space_constraint(a, pltpu.HBM) for a in (slab_green, coupling, left_lead_surface, sigma_right)])

    in_specs = (
        P(None, ("energy", "slab"), None, None),
        P(None, ("energy", "slab"), None, None),
        P("energy", None, None),
        P("energy", None, None),
    )
    out_specs = P(None, ("energy", "slab"), None, None)
    return jax.shard_map(local, mesh=mesh, in_specs=in_specs, out_specs=out_specs, check_vma=False)
```

```python
import functools

import jax
import jax.numpy as jnp
from jax import lax
from jax.experimental import pallas as pl
from jax.experimental.pallas import tpu as pltpu
from jax.sharding import PartitionSpec as P

MESH = pl.DeviceIdType.MESH
BF = jnp.bfloat16
F32 = jnp.float32


def wide(value):
    return jnp.concatenate([value[0], value[1]], axis=1)


def halves(out):
    width = out.shape[1] // 2
    return out[:, :width], out[:, width:]


def low(value):
    return value[0].astype(BF), value[1].astype(BF)


def plus(a, b):
    return a[0] + b[0], a[1] + b[1]


def times(rows, right):
    weights = jnp.concatenate(
        [wide(right), jnp.concatenate([-right[1], right[0]], axis=1)], axis=0
    )
    return jnp.dot(rows, weights, preferred_element_type=F32)


def times_transpose(rows, right):
    weights = jnp.concatenate(
        [
            jnp.concatenate([right[0], -right[1]], axis=1),
            jnp.concatenate([right[1], right[0]], axis=1),
        ],
        axis=0,
    )
    return lax.dot_general(rows, weights, (((1,), (1,)), ((), ())), preferred_element_type=F32)


def product(a, b):
    return low(halves(times(wide(a), b)))


def sandwich(factor, middle):
    inner = times(wide(factor), low(middle)).astype(BF)
    return halves(times_transpose(inner, factor))


def get(ref, *index):
    return ref[(*index, 0)], ref[(*index, 1)]


def put(ref, value, *index):
    ref[(*index, 0)] = value[0].astype(ref.dtype)
    ref[(*index, 1)] = value[1].astype(ref.dtype)


def kernel(
    rounds,
    green_hbm,
    link_hbm,
    lead_hbm,
    sigma_hbm,
    out,
    green,
    link,
    lead,
    sigma,
    own,
    pair,
    given,
    board,
    factors,
    base,
    inbox,
    outbox,
    ends,
    send_sem,
    recv_sem,
    load_sem,
):
    loads = [
        pltpu.make_async_copy(source, target, load_sem.at[k])
        for k, (source, target) in enumerate(
            [(green_hbm, green), (link_hbm, link), (lead_hbm, lead), (sigma_hbm, sigma)]
        )
    ]
    for load in loads:
        load.start()
    layers, width = green.shape[1], green.shape[2]
    energy, me = lax.axis_index("energy"), lax.axis_index("slab")
    role, chip = me % 2, me // 2
    mate = me + 1 - 2 * role
    bit = chip % 2
    side = (bit + role) % 2
    pal = me + (1 - 2 * bit) * 2
    steps = rounds - 1
    spot = chip // 2
    place = spot + role * (2**steps - 1 - 2 * spot)
    stride = (1 - 2 * role) * 4
    lows = [place // 2 ** (k + 1) * 2 ** (k + 1) for k in range(steps)]
    gives = [place == lows[k] + 2**k - 1 for k in range(steps)]
    takes = [(place // 2**k) % 2 == 1 for k in range(steps)]
    givers = [me + stride * (lows[k] + 2**k - 1 - place) for k in range(steps)]

    barrier = pltpu.get_barrier_semaphore()

    def greet(other):
        pl.semaphore_signal(barrier, inc=1, device_id=(energy, other), device_id_type=MESH)

    expected = 2
    greet(mate)
    greet(pal)
    for k in range(steps):
        expected = expected + jnp.where(gives[k], 2**k, 0) + jnp.where(takes[k], 1, 0)

        @pl.when(gives[k])
        def _():
            for d in range(2**k):
                greet(me + stride * (1 + d))

        @pl.when(takes[k])
        def _():
            greet(givers[k])

    def remote(source, target, other, sender, receiver):
        return pltpu.make_async_remote_copy(
            src_ref=source,
            dst_ref=target,
            send_sem=send_sem.at[sender],
            recv_sem=recv_sem.at[receiver],
            device_id=(energy, other),
            device_id_type=MESH,
        )

    zeros = jnp.zeros((width, width), BF)
    for k in range(steps):

        @pl.when(jnp.logical_not(takes[k]))
        def _():
            put(inbox, (zeros, zeros), k, 1)

        @pl.when(jnp.logical_or(jnp.logical_not(takes[k]), lows[k] == 0))
        def _():
            put(inbox, (zeros, zeros), k, 0)

    for load in loads:
        load.wait()
    g = [(green[0, i], green[1, i]) for i in range(layers)]
    c = [(link[0, i], link[1, i]) for i in range(layers)]
    ahead = [low(halves(times_transpose(wide(g[i]), c[i]))) for i in range(layers)]
    back = [product(c[i], g[i]) for i in range(layers)]
    hop = [halves(times_transpose(wide(back[i]), c[i])) for i in range(layers)]

    def merged(first, second):
        return (
            product(second[0], first[0]),
            plus(sandwich(second[0], first[1]), second[1]),
        )

    def whole(items):
        while len(items) > 1:
            rest = items[len(items) // 2 * 2 :]
            items = [merged(*items[k : k + 2]) for k in range(0, len(items) - 1, 2)] + rest
        return items[0]

    up = [(ahead[i], g[i]) for i in range(layers)]
    down = [(back[i], hop[i]) for i in reversed(range(layers))]
    up_total, down_total = whole(up), whole(down)

    put(own, up_total[0], role, 0)
    put(own, up_total[1], role, 1)
    put(own, down_total[0], 1 - role, 0)
    put(own, down_total[1], 1 - role, 1)
    pl.semaphore_wait(barrier, expected)
    swap = remote(own.at[1], pair, mate, 0, 0)
    swap.start()

    up_part, down_part = [up[0]], [down[0]]
    for i in range(1, layers):
        up_part.append(merged(up_part[-1], up[i]) if i + 1 < layers else up_total)
        if i + 1 < layers:
            down_part.append(merged(down_part[-1], down[i]))
    for i in range(layers):
        m_part, s_part = up_part[i]
        put(factors, m_part, role, i)
        if i + 1 < layers:
            m_rest, s_rest = down_part[layers - 2 - i]
            put(factors, product(g[i], m_rest), 1 - role, i)
            put(base, plus(s_part, sandwich(g[i], s_rest)), i)
        else:
            put(factors, g[i], 1 - role, i)
            put(base, s_part, i)

    swap.wait_recv()
    last = 2 + 2 * steps
    hint = remote(own.at[0], given, mate, 2 * 2**steps + 1, last + 1)
    hint.start()
    total = merged((get(own, 0, 0), get(own, 0, 1)), (get(pair, 0), get(pair, 1)))
    forward = role == 0
    start = (
        jnp.where(forward, lead[0], sigma[0]),
        jnp.where(forward, lead[1], sigma[1]),
    )
    row = lax.broadcasted_iota(jnp.int32, (width, width), 0)
    column = lax.broadcasted_iota(jnp.int32, (width, width), 1)
    square = jnp.where(row == column, 1.0, 0.0).astype(BF)

    def wider(value):
        return value[0].astype(F32), value[1].astype(F32)

    def pick(test, a, b):
        return jnp.where(test, a[0], b[0]), jnp.where(test, a[1], b[1])

    def choose(test, a, b):
        return pick(test, a[0], b[0]), pick(test, a[1], b[1])

    put(board, total[0], side, 0)
    put(board, total[1], side, 1)
    cross = remote(board.at[side], board.at[side], pal, 1, 1)
    cross.start()
    cross.wait_recv()
    first = (get(board, 0, 0), wider(get(board, 0, 1)))
    second = (get(board, 1, 0), wider(get(board, 1, 1)))
    total = merged(first, second)
    none = (zeros, zeros)
    head = place == 0

    def settled(value):
        return pick(head, none, value[0]), pick(
            head, plus(sandwich(value[0], start), value[1]), value[1]
        )

    total = settled(total)

    def deliveries(k):
        found = []
        for d in range(2**k):
            other = me + stride * (1 + d)
            at = 2 + 2 * (2**k - 1 + d)
            found.append(
                (
                    remote(outbox.at[k, 1], inbox.at[k, 1], other, at, 2 + 2 * k),
                    remote(outbox.at[k, 0], inbox.at[k, 0], other, at + 1, 3 + 2 * k),
                )
            )
        return found

    def send(k):
        @pl.when(gives[k])
        def _():
            put(outbox, total[1], k, 1)
            put(outbox, total[0], k, 0)
            sent = deliveries(k)
            for constant, _ in sent:
                constant.start()
            if k + 1 < steps:

                @pl.when(lows[k] != 0)
                def _():
                    for _, linear in sent:
                        linear.start()

    def receive(k):
        @pl.when(takes[k])
        def _():
            constant, linear = deliveries(k)[0]
            constant.wait_recv()
            if k + 1 < steps:

                @pl.when(lows[k] != 0)
                def _():
                    linear.wait_recv()

        return get(inbox, k, 0), wider(get(inbox, k, 1))

    def finish(k):
        @pl.when(gives[k])
        def _():
            sent = deliveries(k)
            for constant, _ in sent:
                constant.wait_send()
            if k + 1 < steps:

                @pl.when(lows[k] != 0)
                def _():
                    for _, linear in sent:
                        linear.wait_send()

    if steps:
        send(0)
    before = settled(
        (
            pick(side == 1, first[0], (square, zeros)),
            pick(side == 1, first[1], wider(none)),
        )
    )
    def fold():
        hint.wait_recv()
        parts = [get(factors, 1, i) for i in range(layers)]
        rows = jnp.concatenate([wide(part) for part in parts], axis=0)
        linear = times(rows, get(given, 0))
        inner = times(rows, get(given, 1)).astype(BF)
        for i in range(layers):
            cut = slice(i * width, (i + 1) * width)
            put(base, plus(get(base, i), halves(times_transpose(inner[cut], parts[i]))), i)
            put(factors, halves(linear[cut]), 1, i)

    if not steps:
        fold()
    for k in range(steps):
        if k + 1 == steps:
            fold()
        got = receive(k)
        if k + 1 < steps:
            total = choose(takes[k], merged(got, total), total)
            send(k + 1)
        before = choose(takes[k], merged(got, before), before)
    entering = before[1]
    put(ends, entering, role)
    share = remote(ends.at[role], ends.at[role], mate, 2 * 2**steps, last)
    share.start()

    def spread(k, middle):
        rows = jnp.concatenate([wide(get(factors, k, i)) for i in range(layers)], axis=0)
        inner = times(rows, low(middle)).astype(BF)
        return [
            halves(times_transpose(inner[i * width : (i + 1) * width], get(factors, k, i)))
            for i in range(layers)
        ]

    mine = spread(0, entering)
    for i in range(layers):
        put(base, plus(get(base, i), mine[i]), i)
    share.wait_recv()
    theirs = spread(1, get(ends, 1 - role))
    for i in range(layers):
        value = plus(get(base, i), theirs[i])
        out[0, i] = value[0]
        out[1, i] = value[1]

    swap.wait_send()
    hint.wait_send()
    cross.wait_send()
    share.wait_send()
    for k in range(steps):
        finish(k)


def solution(mesh):
    peers = mesh.shape["slab"]
    rounds = (peers // 2).bit_length() - 1

    def local(slab_green, coupling, left_lead_surface, sigma_right):
        layers, width = slab_green.shape[1], slab_green.shape[2]
        vmem = pl.BlockSpec(memory_space=pltpu.VMEM)
        block = (2, width, width)
        return pl.pallas_call(
            functools.partial(kernel, rounds),
            out_shape=jax.ShapeDtypeStruct(slab_green.shape, F32),
            in_specs=[pl.BlockSpec(memory_space=pltpu.HBM)] * 4,
            out_specs=vmem,
            scratch_shapes=[
                pltpu.VMEM(slab_green.shape, BF),
                pltpu.VMEM(coupling.shape, BF),
                pltpu.VMEM(block, BF),
                pltpu.VMEM(block, BF),
                pltpu.VMEM((2, 2, *block), BF),
                pltpu.VMEM((2, *block), BF),
                pltpu.VMEM((2, *block), BF),
                pltpu.VMEM((2, 2, *block), BF),
                pltpu.VMEM((2, layers, *block), BF),
                pltpu.VMEM((layers, *block), F32),
                pltpu.VMEM((max(rounds - 1, 1), 2, *block), BF),
                pltpu.VMEM((max(rounds - 1, 1), 2, *block), BF),
                pltpu.VMEM((2, *block), BF),
                pltpu.SemaphoreType.DMA((2**rounds + 2,)),
                pltpu.SemaphoreType.DMA((2 * rounds + 2,)),
                pltpu.SemaphoreType.DMA((4,)),
            ],
            compiler_params=pltpu.CompilerParams(collective_id=0, has_side_effects=True, vmem_limit_bytes=16777216),
        )(*[pltpu.with_memory_space_constraint(a, pltpu.HBM) for a in (slab_green, coupling, left_lead_surface, sigma_right)])

    in_specs = (
        P(None, ("energy", "slab"), None, None),
        P(None, ("energy", "slab"), None, None),
        P("energy", None, None),
        P("energy", None, None),
    )
    out_specs = P(None, ("energy", "slab"), None, None)
    return jax.shard_map(local, mesh=mesh, in_specs=in_specs, out_specs=out_specs, check_vma=False)
```

```python
import functools

import jax
import jax.numpy as jnp
from jax import lax
from jax.experimental import pallas as pl
from jax.experimental.pallas import tpu as pltpu
from jax.sharding import PartitionSpec as P

MESH = pl.DeviceIdType.MESH
BF = jnp.bfloat16
F32 = jnp.float32


def wide(value):
    return jnp.concatenate([value[0], value[1]], axis=1)


def halves(out):
    width = out.shape[1] // 2
    return out[:, :width], out[:, width:]


def low(value):
    return value[0].astype(BF), value[1].astype(BF)


def plus(a, b):
    return a[0] + b[0], a[1] + b[1]


def times(rows, right):
    weights = jnp.concatenate(
        [wide(right), jnp.concatenate([-right[1], right[0]], axis=1)], axis=0
    )
    return jnp.dot(rows, weights, preferred_element_type=F32)


def times_transpose(rows, right):
    weights = jnp.concatenate(
        [
            jnp.concatenate([right[0], -right[1]], axis=1),
            jnp.concatenate([right[1], right[0]], axis=1),
        ],
        axis=0,
    )
    return lax.dot_general(rows, weights, (((1,), (1,)), ((), ())), preferred_element_type=F32)


def product(a, b):
    return low(halves(times(wide(a), b)))


def sandwich(factor, middle):
    inner = times(wide(factor), low(middle)).astype(BF)
    return halves(times_transpose(inner, factor))


def get(ref, *index):
    return ref[(*index, 0)], ref[(*index, 1)]


def put(ref, value, *index):
    ref[(*index, 0)] = value[0].astype(ref.dtype)
    ref[(*index, 1)] = value[1].astype(ref.dtype)


def kernel(
    rounds,
    green_hbm,
    link_hbm,
    lead_hbm,
    sigma_hbm,
    out,
    green,
    link,
    lead,
    sigma,
    own,
    pair,
    given,
    board,
    factors,
    base,
    inbox,
    outbox,
    ends,
    send_sem,
    recv_sem,
    load_sem,
):
    loads = [
        pltpu.make_async_copy(source, target, load_sem.at[k])
        for k, (source, target) in enumerate(
            [(green_hbm, green), (link_hbm, link), (lead_hbm, lead), (sigma_hbm, sigma)]
        )
    ]
    for load in loads:
        load.start()
    layers, width = green.shape[1], green.shape[2]
    energy, me = lax.axis_index("energy"), lax.axis_index("slab")
    role, chip = me % 2, me // 2
    mate = me + 1 - 2 * role
    bit = chip % 2
    side = (bit + role) % 2
    pal = me + (1 - 2 * bit) * 2
    steps = rounds - 1
    spot = chip // 2
    place = spot + role * (2**steps - 1 - 2 * spot)
    stride = (1 - 2 * role) * 4
    lows = [place // 2 ** (k + 1) * 2 ** (k + 1) for k in range(steps)]
    gives = [place == lows[k] + 2**k - 1 for k in range(steps)]
    takes = [(place // 2**k) % 2 == 1 for k in range(steps)]
    givers = [me + stride * (lows[k] + 2**k - 1 - place) for k in range(steps)]

    barrier = pltpu.get_barrier_semaphore()

    def greet(other):
        pl.semaphore_signal(barrier, inc=1, device_id=(energy, other), device_id_type=MESH)

    expected = 2
    greet(mate)
    greet(pal)
    for k in range(steps):
        expected = expected + jnp.where(gives[k], 2**k, 0) + jnp.where(takes[k], 1, 0)

        @pl.when(gives[k])
        def _():
            for d in range(2**k):
                greet(me + stride * (1 + d))

        @pl.when(takes[k])
        def _():
            greet(givers[k])

    def remote(source, target, other, sender, receiver):
        return pltpu.make_async_remote_copy(
            src_ref=source,
            dst_ref=target,
            send_sem=send_sem.at[sender],
            recv_sem=recv_sem.at[receiver],
            device_id=(energy, other),
            device_id_type=MESH,
        )

    zeros = jnp.zeros((width, width), BF)
    for k in range(steps):

        @pl.when(jnp.logical_not(takes[k]))
        def _():
            put(inbox, (zeros, zeros), k, 1)

        @pl.when(jnp.logical_or(jnp.logical_not(takes[k]), lows[k] == 0))
        def _():
            put(inbox, (zeros, zeros), k, 0)

    for load in loads[:2]:
        load.wait()
    g = [(green[0, i], green[1, i]) for i in range(layers)]
    c = [(link[0, i], link[1, i]) for i in range(layers)]
    ahead = [low(halves(times_transpose(wide(g[i]), c[i]))) for i in range(layers)]
    back = [product(c[i], g[i]) for i in range(layers)]
    hop = [halves(times_transpose(wide(back[i]), c[i])) for i in range(layers)]

    def merged(first, second):
        return (
            product(second[0], first[0]),
            plus(sandwich(second[0], first[1]), second[1]),
        )

    def whole(items):
        while len(items) > 1:
            rest = items[len(items) // 2 * 2 :]
            items = [merged(*items[k : k + 2]) for k in range(0, len(items) - 1, 2)] + rest
        return items[0]

    up = [(ahead[i], g[i]) for i in range(layers)]
    down = [(back[i], hop[i]) for i in reversed(range(layers))]
    up_total, down_total = whole(up), whole(down)

    put(own, up_total[0], role, 0)
    put(own, up_total[1], role, 1)
    put(own, down_total[0], 1 - role, 0)
    put(own, down_total[1], 1 - role, 1)
    pl.semaphore_wait(barrier, expected)
    swap = remote(own.at[1], pair, mate, 0, 0)
    swap.start()

    up_part, down_part = [up[0]], [down[0]]
    for i in range(1, layers):
        up_part.append(merged(up_part[-1], up[i]) if i + 1 < layers else up_total)
        if i + 1 < layers:
            down_part.append(merged(down_part[-1], down[i]))
    for i in range(layers):
        m_part, s_part = up_part[i]
        put(factors, m_part, role, i)
        if i + 1 < layers:
            m_rest, s_rest = down_part[layers - 2 - i]
            put(factors, product(g[i], m_rest), 1 - role, i)
            put(base, plus(s_part, sandwich(g[i], s_rest)), i)
        else:
            put(factors, g[i], 1 - role, i)
            put(base, s_part, i)

    for load in loads[2:]:
        load.wait()
    swap.wait_recv()
    last = 2 + 2 * steps
    hint = remote(own.at[0], given, mate, 2 * 2**steps + 1, last + 1)
    hint.start()
    total = merged((get(own, 0, 0), get(own, 0, 1)), (get(pair, 0), get(pair, 1)))
    forward = role == 0
    start = (
        jnp.where(forward, lead[0], sigma[0]),
        jnp.where(forward, lead[1], sigma[1]),
    )
    row = lax.broadcasted_iota(jnp.int32, (width, width), 0)
    column = lax.broadcasted_iota(jnp.int32, (width, width), 1)
    square = jnp.where(row == column, 1.0, 0.0).astype(BF)

    def wider(value):
        return value[0].astype(F32), value[1].astype(F32)

    def pick(test, a, b):
        return jnp.where(test, a[0], b[0]), jnp.where(test, a[1], b[1])

    def choose(test, a, b):
        return pick(test, a[0], b[0]), pick(test, a[1], b[1])

    put(board, total[0], side, 0)
    put(board, total[1], side, 1)
    cross = remote(board.at[side], board.at[side], pal, 1, 1)
    cross.start()
    cross.wait_recv()
    first = (get(board, 0, 0), wider(get(board, 0, 1)))
    second = (get(board, 1, 0), wider(get(board, 1, 1)))
    total = merged(first, second)
    none = (zeros, zeros)
    head = place == 0

    def settled(value):
        return pick(head, none, value[0]), pick(
            head, plus(sandwich(value[0], start), value[1]), value[1]
        )

    total = settled(total)

    def deliveries(k):
        found = []
        for d in range(2**k):
            other = me + stride * (1 + d)
            at = 2 + 2 * (2**k - 1 + d)
            found.append(
                (
                    remote(outbox.at[k, 1], inbox.at[k, 1], other, at, 2 + 2 * k),
                    remote(outbox.at[k, 0], inbox.at[k, 0], other, at + 1, 3 + 2 * k),
                )
            )
        return found

    def send(k):
        @pl.when(gives[k])
        def _():
            put(outbox, total[1], k, 1)
            put(outbox, total[0], k, 0)
            sent = deliveries(k)
            for constant, _ in reversed(sent):
                constant.start()
            if k + 1 < steps:

                @pl.when(lows[k] != 0)
                def _():
                    for _, linear in sent:
                        linear.start()

    def receive(k):
        @pl.when(takes[k])
        def _():
            constant, linear = deliveries(k)[0]
            constant.wait_recv()
            if k + 1 < steps:

                @pl.when(lows[k] != 0)
                def _():
                    linear.wait_recv()

        return get(inbox, k, 0), wider(get(inbox, k, 1))

    def finish(k):
        @pl.when(gives[k])
        def _():
            sent = deliveries(k)
            for constant, _ in sent:
                constant.wait_send()
            if k + 1 < steps:

                @pl.when(lows[k] != 0)
                def _():
                    for _, linear in sent:
                        linear.wait_send()

    if steps:
        send(0)
    before = settled(
        (
            pick(side == 1, first[0], (square, zeros)),
            pick(side == 1, first[1], wider(none)),
        )
    )
    hint.wait_recv()
    for i in range(layers):
        factor = get(factors, 1, i)
        put(base, plus(get(base, i), sandwich(factor, get(given, 1))), i)
        put(factors, product(factor, get(given, 0)), 1, i)
    for k in range(steps):
        got = receive(k)
        if k + 1 < steps:
            total = choose(takes[k], merged(got, total), total)
            send(k + 1)
        before = choose(takes[k], merged(got, before), before)
    entering = before[1]
    put(ends, entering, role)
    share = remote(ends.at[role], ends.at[role], mate, 2 * 2**steps, last)
    share.start()

    def spread(k, middle):
        rows = jnp.concatenate([wide(get(factors, k, i)) for i in range(layers)], axis=0)
        inner = times(rows, low(middle)).astype(BF)
        return [
            halves(times_transpose(inner[i * width : (i + 1) * width], get(factors, k, i)))
            for i in range(layers)
        ]

    mine = spread(0, entering)
    for i in range(layers):
        put(base, plus(get(base, i), mine[i]), i)
    share.wait_recv()
    theirs = spread(1, get(ends, 1 - role))
    for i in range(layers):
        value = plus(get(base, i), theirs[i])
        out[0, i] = value[0]
        out[1, i] = value[1]

    swap.wait_send()
    hint.wait_send()
    cross.wait_send()
    share.wait_send()
    for k in range(steps):
        finish(k)


def solution(mesh):
    peers = mesh.shape["slab"]
    rounds = (peers // 2).bit_length() - 1

    def local(slab_green, coupling, left_lead_surface, sigma_right):
        layers, width = slab_green.shape[1], slab_green.shape[2]
        vmem = pl.BlockSpec(memory_space=pltpu.VMEM)
        block = (2, width, width)
        return pl.pallas_call(
            functools.partial(kernel, rounds),
            out_shape=jax.ShapeDtypeStruct(slab_green.shape, F32),
            in_specs=[pl.BlockSpec(memory_space=pltpu.HBM)] * 4,
            out_specs=vmem,
            scratch_shapes=[
                pltpu.VMEM(slab_green.shape, BF),
                pltpu.VMEM(coupling.shape, BF),
                pltpu.VMEM(block, BF),
                pltpu.VMEM(block, BF),
                pltpu.VMEM((2, 2, *block), BF),
                pltpu.VMEM((2, *block), BF),
                pltpu.VMEM((2, *block), BF),
                pltpu.VMEM((2, 2, *block), BF),
                pltpu.VMEM((2, layers, *block), BF),
                pltpu.VMEM((layers, *block), F32),
                pltpu.VMEM((max(rounds - 1, 1), 2, *block), BF),
                pltpu.VMEM((max(rounds - 1, 1), 2, *block), BF),
                pltpu.VMEM((2, *block), BF),
                pltpu.SemaphoreType.DMA((2**rounds + 2,)),
                pltpu.SemaphoreType.DMA((2 * rounds + 2,)),
                pltpu.SemaphoreType.DMA((4,)),
            ],
            compiler_params=pltpu.CompilerParams(collective_id=0, has_side_effects=True, vmem_limit_bytes=16777216),
        )(*[pltpu.with_memory_space_constraint(a, pltpu.HBM) for a in (slab_green, coupling, left_lead_surface, sigma_right)])

    in_specs = (
        P(None, ("energy", "slab"), None, None),
        P(None, ("energy", "slab"), None, None),
        P("energy", None, None),
        P("energy", None, None),
    )
    out_specs = P(None, ("energy", "slab"), None, None)
    return jax.shard_map(local, mesh=mesh, in_specs=in_specs, out_specs=out_specs, check_vma=False)
```
